512 devices in a mesh: energy: 32 (over z_lo, y), slab: 16 (over x, z_hi, core).
Axes of the slice: x: 4, y: 8, z: 8 (z_hi: 2, z_lo: 4; z = z_hi * 4 + z_lo), core: 2. Of those that a mesh axis runs over, the one named last changes fastest.
Arguments:
- green_blocks: bfloat16 [64, 16, 512, 512], P('energy', 'slab'), may hold values from -6 to 6
- coupling: bfloat16 [16, 512, 512], P('slab'), may hold values from -0.25 to 0.25
- coulomb: bfloat16 [16, 512, 512], P('slab'), may hold values from -0.25 to 0.25
Outputs:
- self_energy: bfloat16 [64, 16, 512, 512], P('energy', 'slab')
- screening: bfloat16 [64, 16, 512, 512], P('energy', 'slab')
The draws below stay inside these ranges and needn't reach their ends.
All inputs are finite; a program needn't handle non-finite values.
Results may differ from the reference program's by a relative error of at most 0.0075.
Values may be sent and summed in bfloat16 or wider, within the bound.
No kernel may reach another device: no remote copies, remote signals or barrier semaphores. Data moves between devices by JAX's collectives and lax.ppermute only.
A program may use at most 64 MiB of HBM per device.

```python
import math
import jax
import jax.numpy as jnp
from jax import lax

M = 512
NE = 64
SLABS = 16


def levels(own_key, extent, cuts, smallest, largest):
    factor_of, own = 1.0, jax.random.fold_in(own_key, 6)
    for axis_at, shards_of in cuts:
        steps = jnp.exp(jax.random.uniform(jax.random.fold_in(own, axis_at), (shards_of,), jnp.float32, smallest / len(cuts), largest / len(cuts)))
        factor_of = factor_of * jnp.repeat(steps, extent[axis_at] // shards_of).reshape([-1 if axis == axis_at else 1 for axis in range(len(extent))])
    return factor_of


def noise(key, shape, width, bound, shards=(), kind=jnp.bfloat16):
    loudness = levels(key, shape, shards, -0.22, 0.18) if shards else 1.0
    array = jax.random.normal(key, shape, jnp.float32) * width * loudness
    return jnp.minimum(jnp.maximum(array, -bound), bound).astype(kind)


def setup_inputs(seed: int = 0) -> dict:
    key_of = jax.random.split(jax.random.key(seed), 4)
    return {
        "green_blocks": noise(key_of[0], (NE, SLABS, M, M), 1.0, 6.0, ((0, 32), (1, 16))),
        "coupling": noise(key_of[1], (SLABS, M, M), M ** -0.5, 0.25, ((0, 16),)),
        "coulomb": noise(key_of[2], (SLABS, M, M), M ** -0.5, 0.25, ((0, 16),)),
    }


def tables(count):
    indices = jnp.arange(count, dtype=jnp.int32)
    product = indices[:, None] * indices[None, :] % count
    angles = product.astype(jnp.float32) * (2.0 * math.pi / count)
    return (jnp.cos(angles), jnp.sin(angles))

def correlate(blocks):
    count = blocks.shape[0]
    cosine, sine = tables(count)
    flattened = blocks.astype(jnp.float32).reshape(count, -1)
    cosine_part = jnp.dot(cosine, flattened, precision=lax.Precision.HIGHEST)
    sine_part = jnp.dot(sine, flattened, precision=lax.Precision.HIGHEST)
    spectrum = cosine_part * cosine_part + sine_part * sine_part
    folded = jnp.dot(cosine, spectrum, precision=lax.Precision.HIGHEST) * (1.0 / (count * math.sqrt(count)))
    return folded.reshape(blocks.shape).astype(jnp.bfloat16)

def dress_lower(blocks, link):
    inner = jnp.einsum('eij,jk->eik', blocks.astype(jnp.float32), link.astype(jnp.float32)).astype(jnp.bfloat16)
    return jnp.einsum('ji,ejk->eik', link.astype(jnp.float32), inner.astype(jnp.float32)).astype(jnp.bfloat16)

def dress_upper(blocks, link):
    inner = jnp.einsum('eij,kj->eik', blocks.astype(jnp.float32), link.astype(jnp.float32)).astype(jnp.bfloat16)
    return jnp.einsum('ij,ejk->eik', link.astype(jnp.float32), inner.astype(jnp.float32)).astype(jnp.bfloat16)

def reference(green_blocks, coupling, coulomb):
    slab_ids = jnp.arange(SLABS, dtype=jnp.int32)

    def polar_slab(slab):
        return correlate(lax.dynamic_index_in_dim(green_blocks, slab, 1, False))
    polar = lax.map(polar_slab, slab_ids)

    def per_slab(slab):
        below = jnp.maximum(slab - 1, 0).astype(jnp.int32)
        above = jnp.minimum(slab + 1, SLABS - 1).astype(jnp.int32)
        has_below = (slab > 0).astype(jnp.float32)
        has_above = (slab < SLABS - 1).astype(jnp.float32)
        green_below = lax.dynamic_index_in_dim(green_blocks, below, 1, False)
        green_above = lax.dynamic_index_in_dim(green_blocks, above, 1, False)
        link_below = lax.dynamic_index_in_dim(coupling, below, 0, False)
        link_own = lax.dynamic_index_in_dim(coupling, slab, 0, False)
        lower = dress_lower(green_below, link_below).astype(jnp.float32) * has_below
        upper = dress_upper(green_above, link_own).astype(jnp.float32) * has_above
        sigma = (lower + upper).astype(jnp.bfloat16)
        polar_own = lax.dynamic_index_in_dim(polar, slab, 0, False)
        polar_below = lax.dynamic_index_in_dim(polar, below, 0, False).astype(jnp.float32) * has_below
        polar_above = lax.dynamic_index_in_dim(polar, above, 0, False).astype(jnp.float32) * has_above
        screen_block = lax.dynamic_index_in_dim(coulomb, slab, 0, False).astype(jnp.float32)
        inner = jnp.einsum('eij,kj->eik', polar_own.astype(jnp.float32), screen_block).astype(jnp.bfloat16)
        outer = jnp.einsum('ij,ejk->eik', screen_block, inner.astype(jnp.float32))
        screened = (outer + 0.5 * (polar_below + polar_above)).astype(jnp.bfloat16)
        return (sigma, screened)
    sigmas, screens = lax.map(per_slab, slab_ids)
    return (jnp.swapaxes(sigmas, 0, 1), jnp.swapaxes(screens, 0, 1))
```

```python
import functools
import math

import jax
import jax.numpy as jnp
from jax import lax
from jax.experimental import pallas as pl
from jax.experimental.pallas import tpu as pltpu
from jax.sharding import PartitionSpec as P

F32, BF16 = jnp.float32, jnp.bfloat16
NE, SLABS, M = 64, 16, 512
ENERGY, Z_LO, Y = 32, 4, 8
ROWS = M // ENERGY
BOTH = ("energy", "slab")


def at(energy, slab):
    return energy * SLABS + slab


def along_slabs(block, step):
    route = [(s, s + step) for s in range(SLABS) if 0 <= s + step < SLABS]
    return lax.ppermute(block, "slab", route)


def home_and_across(rows):
    groups = [
        [at(e, s % SLABS) for s in (first, first + 1) for e in range(ENERGY)]
        for first in range(1, SLABS, 2)
    ]
    both = jnp.concatenate([rows, rows], axis=0)
    got = lax.all_to_all(both, BOTH, 0, 0, axis_index_groups=groups, tiled=True)
    return got.reshape(2, *rows.shape)


def on_chip(block):
    return lax.ppermute(block, "slab", [(s, s ^ 1) for s in range(SLABS)])


def dot(a, b, ca, cb):
    return lax.dot_general(a, b, (((ca,), (cb,)), ((), ())), preferred_element_type=F32)


def by_rows(green):
    return jnp.swapaxes(green.reshape(2, ENERGY, ROWS, M), 0, 1)


def lower_kernel(g_ref, h_ref, o_ref):
    inner = dot(g_ref[0], h_ref[...], 1, 0).astype(BF16)
    o_ref[0] = dot(h_ref[...], inner, 0, 0).astype(BF16)


def dress_lower(green, link):
    return pl.pallas_call(
        lower_kernel,
        out_shape=jax.ShapeDtypeStruct((2, M, M), BF16),
        grid=(2,),
        in_specs=[
            pl.BlockSpec((1, M, M), lambda e: (e, 0, 0)),
            pl.BlockSpec((M, M), lambda e: (0, 0)),
        ],
        out_specs=pl.BlockSpec((1, M, M), lambda e: (e, 0, 0)),
        cost_estimate=pl.CostEstimate(
            flops=8 * M**3, bytes_accessed=5 << 19, transcendentals=0
        ),
    )(green, link)


def sigma_kernel(g_ref, h_ref, l_ref, o_ref):
    inner = dot(g_ref[0], h_ref[...], 1, 1).astype(BF16)
    upper = dot(h_ref[...], inner, 1, 0).astype(BF16)
    o_ref[0] = (l_ref[0].astype(F32) + upper.astype(F32)).astype(BF16)


def dress_upper_and_add(green_above, link, lower):
    block = pl.BlockSpec((1, M, M), lambda e: (e, 0, 0))
    return pl.pallas_call(
        sigma_kernel,
        out_shape=jax.ShapeDtypeStruct((2, M, M), BF16),
        grid=(2,),
        in_specs=[block, pl.BlockSpec((M, M), lambda e: (0, 0)), block],
        out_specs=block,
        cost_estimate=pl.CostEstimate(
            flops=8 * M**3, bytes_accessed=7 << 19, transcendentals=0
        ),
    )(green_above, link, lower)


def screen_kernel(where, p_ref, b_ref, c_ref, o_ref):
    polar = p_ref[...].reshape(M, M)
    inner = dot(polar, c_ref[...], 1, 1).astype(BF16)
    outer = dot(c_ref[...], inner, 1, 0)
    across = b_ref[...].reshape(M, M).astype(F32)
    o_ref[...] = outer + jnp.where(where[1] > 0, 0.5 * across, 0.0)


def screen(where, got, block):
    return pl.pallas_call(
        screen_kernel,
        out_shape=jax.ShapeDtypeStruct((2, M, M), F32),
        grid_spec=pltpu.PrefetchScalarGridSpec(
            num_scalar_prefetch=1,
            grid=(2,),
            in_specs=[
                pl.BlockSpec((None, ENERGY, None, ROWS, M), lambda w, f: (f[0], 0, w, 0, 0)),
                pl.BlockSpec((None, ENERGY, None, ROWS, M), lambda w, f: (1 - f[0], 0, w, 0, 0)),
                pl.BlockSpec((M, M), lambda w, f: (0, 0)),
            ],
            out_specs=pl.BlockSpec((None, M, M), lambda w, f: (w, 0, 0)),
        ),
        cost_estimate=pl.CostEstimate(flops=8 * M**3, bytes_accessed=9 << 19, transcendentals=0),
    )(where, got, got, block)


def finish_kernel(s_ref, p_ref, o_ref):
    beside = p_ref[...].reshape(M, M).astype(F32)
    o_ref[...] = (s_ref[...] + 0.5 * beside).astype(BF16)


def finish(screened, partner):
    return pl.pallas_call(
        finish_kernel,
        out_shape=jax.ShapeDtypeStruct((2, M, M), BF16),
        grid=(2,),
        in_specs=[
            pl.BlockSpec((None, M, M), lambda w: (w, 0, 0)),
            pl.BlockSpec((ENERGY, None, ROWS, M), lambda w: (0, w, 0, 0)),
        ],
        out_specs=pl.BlockSpec((None, M, M), lambda w: (w, 0, 0)),
        cost_estimate=pl.CostEstimate(flops=4 * M**2, bytes_accessed=4 << 20, transcendentals=0),
    )(screened, partner)


def tables(count):
    indices = jnp.arange(count, dtype=jnp.int32)
    product = indices[:, None] * indices[None, :] % count
    angles = product.astype(F32) * (2.0 * math.pi / count)
    return (jnp.cos(angles), jnp.sin(angles))


def correlate(rows):
    cosine, sine = tables(NE)
    flat = rows.astype(F32).reshape(NE, -1)
    cosine_part = jnp.dot(cosine, flat, precision=lax.Precision.HIGHEST)
    sine_part = jnp.dot(sine, flat, precision=lax.Precision.HIGHEST)
    spectrum = cosine_part * cosine_part + sine_part * sine_part
    folded = jnp.dot(cosine, spectrum, precision=lax.Precision.HIGHEST) * (
        1.0 / (NE * math.sqrt(NE))
    )
    return folded.reshape(rows.shape).astype(BF16)


def on_device(green_blocks, coupling, coulomb):
    green, link, block = green_blocks[:, 0], coupling[0], coulomb[0]
    slab = lax.axis_index("slab")
    own = 1 - (slab & 1)
    across = jnp.where((slab > 0) & (slab < SLABS - 1), 1, 0)
    where = jnp.stack([own, across]).astype(jnp.int32)

    rows = lax.all_to_all(by_rows(green), "energy", 0, 0, tiled=True)
    green_above = along_slabs(green, -1)
    lower = along_slabs(dress_lower(green, link), 1)
    polar_rows = correlate(rows.reshape(NE, ROWS, M))
    polar_rows, lower = lax.optimization_barrier((polar_rows, lower))
    got = home_and_across(polar_rows.reshape(ENERGY, 2, ROWS, M))
    partner = on_chip(lax.dynamic_index_in_dim(got, own, 0, False))
    screened = finish(screen(where, got, block), partner)
    sigma = dress_upper_and_add(green_above, link, lower)
    return (sigma[:, None], screened[:, None])


def solution(mesh):
    placed = (P("energy", "slab", None, None), P("slab", None, None), P("slab", None, None))
    return jax.shard_map(
        on_device,
        mesh=mesh,
        in_specs=placed,
        out_specs=(P("energy", "slab", None, None), P("energy", "slab", None, None)),
        check_vma=False,
    )
```

```python
import functools
import math

import jax
import jax.numpy as jnp
from jax import lax
from jax.experimental import pallas as pl
from jax.experimental.pallas import tpu as pltpu
from jax.sharding import PartitionSpec as P

F32, BF16 = jnp.float32, jnp.bfloat16
NE, SLABS, M = 64, 16, 512
ENERGY, Z_LO, Y = 32, 4, 8
ROWS = M // ENERGY
BOTH = ("energy", "slab")
WIDE = 1000 * M**3


def at(energy, slab):
    return energy * SLABS + slab


def along_slabs(block, step):
    route = [(s, s + step) for s in range(SLABS) if 0 <= s + step < SLABS]
    return lax.ppermute(block, "slab", route)


def home_and_across(rows):
    groups = [
        [at(e, s % SLABS) for s in (first, first + 1) for e in range(ENERGY)]
        for first in range(1, SLABS, 2)
    ]
    both = jnp.concatenate([rows, rows], axis=0)
    got = lax.all_to_all(both, BOTH, 0, 0, axis_index_groups=groups, tiled=True)
    return got.reshape(2, *rows.shape)


def on_chip(block):
    return lax.ppermute(block, "slab", [(s, s ^ 1) for s in range(SLABS)])


def dot(a, b, ca, cb):
    return lax.dot_general(a, b, (((ca,), (cb,)), ((), ())), preferred_element_type=F32)


def by_rows(green):
    return jnp.swapaxes(green.reshape(2, ENERGY, ROWS, M), 0, 1)


def lower_kernel(g_ref, h_ref, o_ref):
    inner = dot(g_ref[0], h_ref[...], 1, 0).astype(BF16)
    o_ref[0] = dot(h_ref[...], inner, 0, 0).astype(BF16)


def dress_lower(green, link):
    return pl.pallas_call(
        lower_kernel,
        out_shape=jax.ShapeDtypeStruct((2, M, M), BF16),
        grid=(2,),
        in_specs=[
            pl.BlockSpec((1, M, M), lambda e: (e, 0, 0)),
            pl.BlockSpec((M, M), lambda e: (0, 0)),
        ],
        out_specs=pl.BlockSpec((1, M, M), lambda e: (e, 0, 0)),
        compiler_params=pltpu.CompilerParams(vmem_limit_bytes=16 << 20),
        cost_estimate=pl.CostEstimate(
            flops=8 * M**3, bytes_accessed=5 << 19, transcendentals=0
        ),
    )(green, link)


def upper_kernel(g_ref, h_ref, o_ref):
    inner = dot(g_ref[0], h_ref[...], 1, 1).astype(BF16)
    o_ref[0] = dot(h_ref[...], inner, 1, 0).astype(BF16)


def dress_upper(green_above, link):
    block = pl.BlockSpec((1, M, M), lambda e: (e, 0, 0))
    return pl.pallas_call(
        upper_kernel,
        out_shape=jax.ShapeDtypeStruct((2, M, M), BF16),
        grid=(2,),
        in_specs=[block, pl.BlockSpec((M, M), lambda e: (0, 0))],
        out_specs=block,
        compiler_params=pltpu.CompilerParams(vmem_limit_bytes=16 << 20),
        cost_estimate=pl.CostEstimate(flops=WIDE, bytes_accessed=5 << 19, transcendentals=0),
    )(green_above, link)


def sum_kernel(a_ref, b_ref, o_ref):
    o_ref[...] = (a_ref[...].astype(F32) + b_ref[...].astype(F32)).astype(BF16)


def added(a, b):
    block = pl.BlockSpec((1, M, M), lambda e: (e, 0, 0))
    return pl.pallas_call(
        sum_kernel,
        out_shape=jax.ShapeDtypeStruct((2, M, M), BF16),
        grid=(2,),
        in_specs=[block, block],
        out_specs=block,
        compiler_params=pltpu.CompilerParams(vmem_limit_bytes=16 << 20),
        cost_estimate=pl.CostEstimate(flops=WIDE, bytes_accessed=3 << 20, transcendentals=0),
    )(a, b)


def screen_kernel(where, p_ref, b_ref, c_ref, o_ref):
    polar = p_ref[...].reshape(M, M)
    inner = dot(polar, c_ref[...], 1, 1).astype(BF16)
    outer = dot(c_ref[...], inner, 1, 0)
    across = b_ref[...].reshape(M, M).astype(F32)
    o_ref[...] = outer + jnp.where(where[1] > 0, 0.5 * across, 0.0)


def screen(where, got, block):
    return pl.pallas_call(
        screen_kernel,
        out_shape=jax.ShapeDtypeStruct((2, M, M), F32),
        grid_spec=pltpu.PrefetchScalarGridSpec(
            num_scalar_prefetch=1,
            grid=(2,),
            in_specs=[
                pl.BlockSpec((None, ENERGY, None, ROWS, M), lambda w, f: (f[0], 0, w, 0, 0)),
                pl.BlockSpec((None, ENERGY, None, ROWS, M), lambda w, f: (1 - f[0], 0, w, 0, 0)),
                pl.BlockSpec((M, M), lambda w, f: (0, 0)),
            ],
            out_specs=pl.BlockSpec((None, M, M), lambda w, f: (w, 0, 0)),
        ),
        compiler_params=pltpu.CompilerParams(vmem_limit_bytes=16 << 20),
        cost_estimate=pl.CostEstimate(flops=8 * M**3, bytes_accessed=9 << 19, transcendentals=0),
    )(where, got, got, block)


def finish_kernel(s_ref, p_ref, o_ref):
    beside = p_ref[...].reshape(M, M).astype(F32)
    o_ref[...] = (s_ref[...] + 0.5 * beside).astype(BF16)


def finish(screened, partner):
    return pl.pallas_call(
        finish_kernel,
        out_shape=jax.ShapeDtypeStruct((2, M, M), BF16),
        grid=(2,),
        in_specs=[
            pl.BlockSpec((None, M, M), lambda w: (w, 0, 0)),
            pl.BlockSpec((ENERGY, None, ROWS, M), lambda w: (0, w, 0, 0)),
        ],
        out_specs=pl.BlockSpec((None, M, M), lambda w: (w, 0, 0)),
        compiler_params=pltpu.CompilerParams(vmem_limit_bytes=16 << 20),
        cost_estimate=pl.CostEstimate(flops=4 * M**2, bytes_accessed=4 << 20, transcendentals=0),
    )(screened, partner)


def tables(count):
    indices = jnp.arange(count, dtype=jnp.int32)
    product = indices[:, None] * indices[None, :] % count
    angles = product.astype(F32) * (2.0 * math.pi / count)
    return (jnp.cos(angles), jnp.sin(angles))


def correlate(rows):
    cosine, sine = tables(NE)
    flat = rows.astype(F32).reshape(NE, -1)
    cosine_part = jnp.dot(cosine, flat, precision=lax.Precision.HIGHEST)
    sine_part = jnp.dot(sine, flat, precision=lax.Precision.HIGHEST)
    spectrum = cosine_part * cosine_part + sine_part * sine_part
    folded = jnp.dot(cosine, spectrum, precision=lax.Precision.HIGHEST) * (
        1.0 / (NE * math.sqrt(NE))
    )
    return folded.reshape(rows.shape).astype(BF16)


def on_device(green_blocks, coupling, coulomb):
    green, link, block = green_blocks[:, 0], coupling[0], coulomb[0]
    slab = lax.axis_index("slab")
    own = 1 - (slab & 1)
    across = jnp.where((slab > 0) & (slab < SLABS - 1), 1, 0)
    where = jnp.stack([own, across]).astype(jnp.int32)

    green_above = along_slabs(green, -1)
    rows = lax.all_to_all(by_rows(green), "energy", 0, 0, tiled=True)
    rows, lower_here, upper, where = lax.optimization_barrier(
        (rows, dress_lower(green, link), dress_upper(green_above, link), where)
    )
    lower = along_slabs(lower_here, 1)
    polar_rows = correlate(rows.reshape(NE, ROWS, M))
    got = home_and_across(polar_rows.reshape(ENERGY, 2, ROWS, M))
    sigma = added(lower, upper)
    got, sigma = lax.optimization_barrier((got, sigma))
    partner = on_chip(lax.dynamic_index_in_dim(got, own, 0, False))
    screened = finish(screen(where, got, block), partner)
    return (sigma[:, None], screened[:, None])


def solution(mesh):
    placed = (P("energy", "slab", None, None), P("slab", None, None), P("slab", None, None))
    return jax.shard_map(
        on_device,
        mesh=mesh,
        in_specs=placed,
        out_specs=(P("energy", "slab", None, None), P("energy", "slab", None, None)),
        check_vma=False,
    )
```

```python
import functools
import math

import jax
import jax.numpy as jnp
from jax import lax
from jax.experimental import pallas as pl
from jax.experimental.pallas import tpu as pltpu
from jax.sharding import PartitionSpec as P

F32, BF16 = jnp.float32, jnp.bfloat16
NE, SLABS, M = 64, 16, 512
ENERGY, Z_LO, Y = 32, 4, 8
ROWS = M // ENERGY
BOTH = ("energy", "slab")
WIDE = 1000 * M**3


def at(energy, slab):
    return energy * SLABS + slab


def along_slabs(block, step):
    route = [(s, s + step) for s in range(SLABS) if 0 <= s + step < SLABS]
    return lax.ppermute(block, "slab", route)


def home_and_across(rows):
    groups = [
        [at(e, s % SLABS) for s in (first, first + 1) for e in range(ENERGY)]
        for first in range(1, SLABS, 2)
    ]
    both = jnp.concatenate([rows, rows], axis=0)
    got = lax.all_to_all(both, BOTH, 0, 0, axis_index_groups=groups, tiled=True)
    return got.reshape(2, *rows.shape)


def on_chip(block):
    return lax.ppermute(block, "slab", [(s, s ^ 1) for s in range(SLABS)])


def dot(a, b, ca, cb):
    return lax.dot_general(a, b, (((ca,), (cb,)), ((), ())), preferred_element_type=F32)


def by_rows(green):
    return jnp.swapaxes(green.reshape(2, ENERGY, ROWS, M), 0, 1)


def lower_kernel(g_ref, h_ref, o_ref):
    inner = dot(g_ref[0], h_ref[...], 1, 0).astype(BF16)
    o_ref[0] = dot(h_ref[...], inner, 0, 0).astype(BF16)


def dress_lower(green, link):
    return pl.pallas_call(
        lower_kernel,
        out_shape=jax.ShapeDtypeStruct((2, M, M), BF16),
        grid=(2,),
        in_specs=[
            pl.BlockSpec((1, M, M), lambda e: (e, 0, 0)),
            pl.BlockSpec((M, M), lambda e: (0, 0)),
        ],
        out_specs=pl.BlockSpec((1, M, M), lambda e: (e, 0, 0)),
        compiler_params=pltpu.CompilerParams(vmem_limit_bytes=16 << 20),
        cost_estimate=pl.CostEstimate(
            flops=8 * M**3, bytes_accessed=5 << 19, transcendentals=0
        ),
    )(green, link)


def upper_kernel(g_ref, h_ref, o_ref):
    inner = dot(g_ref[0], h_ref[...], 1, 1).astype(BF16)
    o_ref[0] = dot(h_ref[...], inner, 1, 0).astype(BF16)


def dress_upper(green_above, link):
    block = pl.BlockSpec((1, M, M), lambda e: (e, 0, 0))
    return pl.pallas_call(
        upper_kernel,
        out_shape=jax.ShapeDtypeStruct((2, M, M), BF16),
        grid=(2,),
        in_specs=[block, pl.BlockSpec((M, M), lambda e: (0, 0))],
        out_specs=block,
        compiler_params=pltpu.CompilerParams(vmem_limit_bytes=16 << 20),
        cost_estimate=pl.CostEstimate(flops=8 * M**3, bytes_accessed=5 << 19, transcendentals=0),
    )(green_above, link)


def sum_kernel(a_ref, b_ref, o_ref):
    o_ref[...] = (a_ref[...].astype(F32) + b_ref[...].astype(F32)).astype(BF16)


def added(a, b):
    block = pl.BlockSpec((1, M, M), lambda e: (e, 0, 0))
    return pl.pallas_call(
        sum_kernel,
        out_shape=jax.ShapeDtypeStruct((2, M, M), BF16),
        grid=(2,),
        in_specs=[block, block],
        out_specs=block,
        compiler_params=pltpu.CompilerParams(vmem_limit_bytes=16 << 20),
        cost_estimate=pl.CostEstimate(flops=2 * M**2, bytes_accessed=3 << 20, transcendentals=0),
    )(a, b)


def after_kernel(arrived_ref, where_ref, o_ref):
    for k in range(2):
        o_ref[k] = where_ref[k]


def after(arrived, where):
    scalars = pl.BlockSpec(memory_space=pltpu.SMEM)
    return pl.pallas_call(
        after_kernel,
        out_shape=jax.ShapeDtypeStruct((2,), jnp.int32),
        in_specs=[pl.BlockSpec(memory_space=pl.ANY), scalars],
        out_specs=scalars,
        compiler_params=pltpu.CompilerParams(vmem_limit_bytes=1 << 20),
        cost_estimate=pl.CostEstimate(flops=WIDE, bytes_accessed=64, transcendentals=0),
    )(arrived, where)


def screen_kernel(where, p_ref, b_ref, c_ref, o_ref):
    polar = p_ref[...].reshape(M, M)
    inner = dot(polar, c_ref[...], 1, 1).astype(BF16)
    outer = dot(c_ref[...], inner, 1, 0)
    across = b_ref[...].reshape(M, M).astype(F32)
    o_ref[...] = outer + jnp.where(where[1] > 0, 0.5 * across, 0.0)


def screen(where, got, block):
    return pl.pallas_call(
        screen_kernel,
        out_shape=jax.ShapeDtypeStruct((2, M, M), F32),
        grid_spec=pltpu.PrefetchScalarGridSpec(
            num_scalar_prefetch=1,
            grid=(2,),
            in_specs=[
                pl.BlockSpec((None, ENERGY, None, ROWS, M), lambda w, f: (f[0], 0, w, 0, 0)),
                pl.BlockSpec((None, ENERGY, None, ROWS, M), lambda w, f: (1 - f[0], 0, w, 0, 0)),
                pl.BlockSpec((M, M), lambda w, f: (0, 0)),
            ],
            out_specs=pl.BlockSpec((None, M, M), lambda w, f: (w, 0, 0)),
        ),
        compiler_params=pltpu.CompilerParams(vmem_limit_bytes=16 << 20),
        cost_estimate=pl.CostEstimate(flops=8 * M**3, bytes_accessed=9 << 19, transcendentals=0),
    )(where, got, got, block)


def finish_kernel(s_ref, p_ref, o_ref):
    beside = p_ref[...].reshape(M, M).astype(F32)
    o_ref[...] = (s_ref[...] + 0.5 * beside).astype(BF16)


def finish(screened, partner):
    return pl.pallas_call(
        finish_kernel,
        out_shape=jax.ShapeDtypeStruct((2, M, M), BF16),
        grid=(2,),
        in_specs=[
            pl.BlockSpec((None, M, M), lambda w: (w, 0, 0)),
            pl.BlockSpec((ENERGY, None, ROWS, M), lambda w: (0, w, 0, 0)),
        ],
        out_specs=pl.BlockSpec((None, M, M), lambda w: (w, 0, 0)),
        compiler_params=pltpu.CompilerParams(vmem_limit_bytes=16 << 20),
        cost_estimate=pl.CostEstimate(flops=4 * M**2, bytes_accessed=4 << 20, transcendentals=0),
    )(screened, partner)


def tables(count):
    indices = jnp.arange(count, dtype=jnp.int32)
    product = indices[:, None] * indices[None, :] % count
    angles = product.astype(F32) * (2.0 * math.pi / count)
    return (jnp.cos(angles), jnp.sin(angles))


def correlate(rows):
    cosine, sine = tables(NE)
    flat = rows.astype(F32).reshape(NE, -1)
    cosine_part = jnp.dot(cosine, flat, precision=lax.Precision.HIGH)
    sine_part = jnp.dot(sine, flat, precision=lax.Precision.HIGH)
    spectrum = cosine_part * cosine_part + sine_part * sine_part
    folded = jnp.dot(cosine, spectrum, precision=lax.Precision.HIGH) * (
        1.0 / (NE * math.sqrt(NE))
    )
    return folded.reshape(rows.shape).astype(BF16)


def on_device(green_blocks, coupling, coulomb):
    green, link, block = green_blocks[:, 0], coupling[0], coulomb[0]
    slab = lax.axis_index("slab")
    own = 1 - (slab & 1)
    across = jnp.where((slab > 0) & (slab < SLABS - 1), 1, 0)
    where = jnp.stack([own, across]).astype(jnp.int32)

    green_above = along_slabs(green, -1)
    rows = lax.all_to_all(by_rows(green), "energy", 0, 0, tiled=True)
    rows, lower_here, where = lax.optimization_barrier(
        (rows, dress_lower(green, link), after(green_above, where))
    )
    lower = along_slabs(lower_here, 1)
    polar_rows = correlate(rows.reshape(NE, ROWS, M))
    polar_rows, green_above = lax.optimization_barrier((polar_rows, green_above))
    got = home_and_across(polar_rows.reshape(ENERGY, 2, ROWS, M))
    sigma = added(lower, dress_upper(green_above, link))
    got, sigma, where = lax.optimization_barrier((got, sigma, after(lower, where)))
    partner = on_chip(lax.dynamic_index_in_dim(got, where[0], 0, False))
    screened = finish(screen(where, got, block), partner)
    return (sigma[:, None], screened[:, None])


def solution(mesh):
    placed = (P("energy", "slab", None, None), P("slab", None, None), P("slab", None, None))
    return jax.shard_map(
        on_device,
        mesh=mesh,
        in_specs=placed,
        out_specs=(P("energy", "slab", None, None), P("energy", "slab", None, None)),
        check_vma=False,
    )
```

```python
import functools
import math

import jax
import jax.numpy as jnp
from jax import lax
from jax.experimental import pallas as pl
from jax.experimental.pallas import tpu as pltpu
from jax.sharding import PartitionSpec as P

F32, BF16 = jnp.float32, jnp.bfloat16
NE, SLABS, M = 64, 16, 512
ENERGY, Z_LO, Y = 32, 4, 8
ROWS = M // ENERGY
BOTH = ("energy", "slab")
WIDE = 1000 * M**3


def at(energy, slab):
    return energy * SLABS + slab


def along_slabs(block, step):
    route = [(s, s + step) for s in range(SLABS) if 0 <= s + step < SLABS]
    return lax.ppermute(block, "slab", route)


def home_and_across(rows):
    groups = [
        [at(e, s % SLABS) for e in range(ENERGY) for s in (first, first + 1)]
        for first in range(1, SLABS, 2)
    ]
    both = jnp.stack([rows, rows], axis=1)
    got = lax.all_to_all(
        both.reshape(2 * ENERGY, *rows.shape[1:]),
        BOTH,
        0,
        0,
        axis_index_groups=groups,
        tiled=True,
    )
    return got.reshape(both.shape)


def on_chip(block):
    return lax.ppermute(block, "slab", [(s, s ^ 1) for s in range(SLABS)])


def dot(a, b, ca, cb):
    return lax.dot_general(a, b, (((ca,), (cb,)), ((), ())), preferred_element_type=F32)


def by_rows(green):
    return jnp.swapaxes(green.reshape(2, ENERGY, ROWS, M), 0, 1)


def lower_kernel(g_ref, h_ref, o_ref):
    inner = dot(g_ref[0], h_ref[...], 1, 0).astype(BF16)
    o_ref[0] = dot(h_ref[...], inner, 0, 0).astype(BF16)


def dress_lower(green, link):
    return pl.pallas_call(
        lower_kernel,
        out_shape=jax.ShapeDtypeStruct((2, M, M), BF16),
        grid=(2,),
        in_specs=[
            pl.BlockSpec((1, M, M), lambda e: (e, 0, 0)),
            pl.BlockSpec((M, M), lambda e: (0, 0)),
        ],
        out_specs=pl.BlockSpec((1, M, M), lambda e: (e, 0, 0)),
        compiler_params=pltpu.CompilerParams(vmem_limit_bytes=16 << 20),
        cost_estimate=pl.CostEstimate(
            flops=8 * M**3, bytes_accessed=5 << 19, transcendentals=0
        ),
    )(green, link)


def upper_kernel(g_ref, h_ref, o_ref):
    inner = dot(g_ref[0], h_ref[...], 1, 1).astype(BF16)
    o_ref[0] = dot(h_ref[...], inner, 1, 0).astype(BF16)


def dress_upper(green_above, link):
    block = pl.BlockSpec((1, M, M), lambda e: (e, 0, 0))
    return pl.pallas_call(
        upper_kernel,
        out_shape=jax.ShapeDtypeStruct((2, M, M), BF16),
        grid=(2,),
        in_specs=[block, pl.BlockSpec((M, M), lambda e: (0, 0))],
        out_specs=block,
        compiler_params=pltpu.CompilerParams(vmem_limit_bytes=16 << 20),
        cost_estimate=pl.CostEstimate(flops=WIDE, bytes_accessed=5 << 19, transcendentals=0),
    )(green_above, link)


def sum_kernel(a_ref, b_ref, o_ref):
    o_ref[...] = (a_ref[...].astype(F32) + b_ref[...].astype(F32)).astype(BF16)


def added(a, b):
    block = pl.BlockSpec((1, M, M), lambda e: (e, 0, 0))
    return pl.pallas_call(
        sum_kernel,
        out_shape=jax.ShapeDtypeStruct((2, M, M), BF16),
        grid=(2,),
        in_specs=[block, block],
        out_specs=block,
        compiler_params=pltpu.CompilerParams(vmem_limit_bytes=16 << 20),
        cost_estimate=pl.CostEstimate(flops=2 * M**2, bytes_accessed=3 << 20, transcendentals=0),
    )(a, b)


def after_kernel(arrived_ref, where_ref, o_ref):
    for k in range(2):
        o_ref[k] = where_ref[k]


def after(arrived, where):
    scalars = pl.BlockSpec(memory_space=pltpu.SMEM)
    return pl.pallas_call(
        after_kernel,
        out_shape=jax.ShapeDtypeStruct((2,), jnp.int32),
        in_specs=[pl.BlockSpec(memory_space=pl.ANY), scalars],
        out_specs=scalars,
        compiler_params=pltpu.CompilerParams(vmem_limit_bytes=1 << 20),
        cost_estimate=pl.CostEstimate(flops=WIDE, bytes_accessed=64, transcendentals=0),
    )(arrived, where)


def screen_kernel(where, p_ref, b_ref, c_ref, o_ref):
    polar = p_ref[...].reshape(M, M)
    inner = dot(polar, c_ref[...], 1, 1).astype(BF16)
    outer = dot(c_ref[...], inner, 1, 0)
    across = b_ref[...].reshape(M, M).astype(F32)
    o_ref[...] = outer + jnp.where(where[1] > 0, 0.5 * across, 0.0)


def screen(where, got, block):
    return pl.pallas_call(
        screen_kernel,
        out_shape=jax.ShapeDtypeStruct((2, M, M), F32),
        grid_spec=pltpu.PrefetchScalarGridSpec(
            num_scalar_prefetch=1,
            grid=(2,),
            in_specs=[
                pl.BlockSpec((ENERGY, None, None, ROWS, M), lambda w, f: (0, f[0], w, 0, 0)),
                pl.BlockSpec((ENERGY, None, None, ROWS, M), lambda w, f: (0, 1 - f[0], w, 0, 0)),
                pl.BlockSpec((M, M), lambda w, f: (0, 0)),
            ],
            out_specs=pl.BlockSpec((None, M, M), lambda w, f: (w, 0, 0)),
        ),
        compiler_params=pltpu.CompilerParams(vmem_limit_bytes=16 << 20),
        cost_estimate=pl.CostEstimate(flops=8 * M**3, bytes_accessed=9 << 19, transcendentals=0),
    )(where, got, got, block)


def finish_kernel(s_ref, p_ref, o_ref):
    beside = p_ref[...].reshape(M, M).astype(F32)
    o_ref[...] = (s_ref[...] + 0.5 * beside).astype(BF16)


def finish(screened, partner):
    return pl.pallas_call(
        finish_kernel,
        out_shape=jax.ShapeDtypeStruct((2, M, M), BF16),
        grid=(2,),
        in_specs=[
            pl.BlockSpec((None, M, M), lambda w: (w, 0, 0)),
            pl.BlockSpec((ENERGY, None, ROWS, M), lambda w: (0, w, 0, 0)),
        ],
        out_specs=pl.BlockSpec((None, M, M), lambda w: (w, 0, 0)),
        compiler_params=pltpu.CompilerParams(vmem_limit_bytes=16 << 20),
        cost_estimate=pl.CostEstimate(flops=4 * M**2, bytes_accessed=4 << 20, transcendentals=0),
    )(screened, partner)


def tables(count):
    indices = jnp.arange(count, dtype=jnp.int32)
    product = indices[:, None] * indices[None, :] % count
    angles = product.astype(F32) * (2.0 * math.pi / count)
    return (jnp.cos(angles), jnp.sin(angles))


def correlate(rows):
    cosine, sine = tables(NE)
    flat = rows.astype(F32).reshape(NE, -1)
    cosine_part = jnp.dot(cosine, flat, precision=lax.Precision.HIGHEST)
    sine_part = jnp.dot(sine, flat, precision=lax.Precision.HIGHEST)
    spectrum = cosine_part * cosine_part + sine_part * sine_part
    folded = jnp.dot(cosine, spectrum, precision=lax.Precision.HIGHEST) * (
        1.0 / (NE * math.sqrt(NE))
    )
    return folded.reshape(rows.shape).astype(BF16)


def on_device(green_blocks, coupling, coulomb):
    green, link, block = green_blocks[:, 0], coupling[0], coulomb[0]
    slab = lax.axis_index("slab")
    own = 1 - (slab & 1)
    across = jnp.where((slab > 0) & (slab < SLABS - 1), 1, 0)
    where = jnp.stack([own, across]).astype(jnp.int32)

    green_above = along_slabs(green, -1)
    rows = lax.all_to_all(by_rows(green), "energy", 0, 0, tiled=True)
    rows, lower_here, upper, where = lax.optimization_barrier(
        (rows, dress_lower(green, link), dress_upper(green_above, link), where)
    )
    lower = along_slabs(lower_here, 1)
    polar_rows = correlate(rows.reshape(NE, ROWS, M))
    got = home_and_across(polar_rows.reshape(ENERGY, 2, ROWS, M))
    sigma = added(lower, upper)
    got, sigma, where = lax.optimization_barrier((got, sigma, after(lower, where)))
    partner = on_chip(lax.dynamic_index_in_dim(got, own, 1, False))
    screened = finish(screen(where, got, block), partner)
    return (sigma[:, None], screened[:, None])


def solution(mesh):
    placed = (P("energy", "slab", None, None), P("slab", None, None), P("slab", None, None))
    return jax.shard_map(
        on_device,
        mesh=mesh,
        in_specs=placed,
        out_specs=(P("energy", "slab", None, None), P("energy", "slab", None, None)),
        check_vma=False,
    )
```

```python
import functools
import math

import jax
import jax.numpy as jnp
from jax import lax
from jax.experimental import pallas as pl
from jax.experimental.pallas import tpu as pltpu
from jax.sharding import PartitionSpec as P

F32, BF16 = jnp.float32, jnp.bfloat16
NE, SLABS, M = 64, 16, 512
ENERGY, Z_LO, Y = 32, 4, 8
ROWS = M // ENERGY
BOTH = ("energy", "slab")
WIDE = 1000 * M**3


Z_FIRST = [z * Y + y for y in range(Y) for z in range(Z_LO)]


def at(energy, slab):
    return energy * SLABS + slab


def along_slabs(block, step):
    route = [(s, s + step) for s in range(SLABS) if 0 <= s + step < SLABS]
    return lax.ppermute(block, "slab", route)


def home_and_across(rows):
    groups = [
        [at(e, s % SLABS) for e in Z_FIRST for s in (first, first + 1)]
        for first in range(1, SLABS, 2)
    ]
    both = jnp.stack([rows, rows], axis=1)
    got = lax.all_to_all(
        both.reshape(2 * ENERGY, *rows.shape[1:]),
        BOTH,
        0,
        0,
        axis_index_groups=groups,
        tiled=True,
    )
    return got.reshape(both.shape)


def on_chip(block):
    return lax.ppermute(block, "slab", [(s, s ^ 1) for s in range(SLABS)])


def dot(a, b, ca, cb):
    return lax.dot_general(a, b, (((ca,), (cb,)), ((), ())), preferred_element_type=F32)


def by_rows(green):
    return jnp.swapaxes(green.reshape(2, ENERGY, ROWS, M), 0, 1)


def lower_kernel(g_ref, h_ref, o_ref):
    inner = dot(g_ref[0], h_ref[...], 1, 0).astype(BF16)
    o_ref[0] = dot(h_ref[...], inner, 0, 0).astype(BF16)


def dress_lower(green, link):
    return pl.pallas_call(
        lower_kernel,
        out_shape=jax.ShapeDtypeStruct((2, M, M), BF16),
        grid=(2,),
        in_specs=[
            pl.BlockSpec((1, M, M), lambda e: (e, 0, 0)),
            pl.BlockSpec((M, M), lambda e: (0, 0)),
        ],
        out_specs=pl.BlockSpec((1, M, M), lambda e: (e, 0, 0)),
        compiler_params=pltpu.CompilerParams(vmem_limit_bytes=16 << 20),
        cost_estimate=pl.CostEstimate(
            flops=8 * M**3, bytes_accessed=5 << 19, transcendentals=0
        ),
    )(green, link)


def upper_kernel(g_ref, h_ref, o_ref):
    inner = dot(g_ref[0], h_ref[...], 1, 1).astype(BF16)
    o_ref[0] = dot(h_ref[...], inner, 1, 0).astype(BF16)


def dress_upper(green_above, link):
    block = pl.BlockSpec((1, M, M), lambda e: (e, 0, 0))
    return pl.pallas_call(
        upper_kernel,
        out_shape=jax.ShapeDtypeStruct((2, M, M), BF16),
        grid=(2,),
        in_specs=[block, pl.BlockSpec((M, M), lambda e: (0, 0))],
        out_specs=block,
        compiler_params=pltpu.CompilerParams(vmem_limit_bytes=16 << 20),
        cost_estimate=pl.CostEstimate(flops=WIDE, bytes_accessed=5 << 19, transcendentals=0),
    )(green_above, link)


def sum_kernel(a_ref, b_ref, o_ref):
    o_ref[...] = (a_ref[...].astype(F32) + b_ref[...].astype(F32)).astype(BF16)


def added(a, b):
    block = pl.BlockSpec((1, M, M), lambda e: (e, 0, 0))
    return pl.pallas_call(
        sum_kernel,
        out_shape=jax.ShapeDtypeStruct((2, M, M), BF16),
        grid=(2,),
        in_specs=[block, block],
        out_specs=block,
        compiler_params=pltpu.CompilerParams(vmem_limit_bytes=16 << 20),
        cost_estimate=pl.CostEstimate(flops=2 * M**2, bytes_accessed=3 << 20, transcendentals=0),
    )(a, b)


def after_kernel(arrived_ref, where_ref, o_ref):
    for k in range(2):
        o_ref[k] = where_ref[k]


def after(arrived, where):
    scalars = pl.BlockSpec(memory_space=pltpu.SMEM)
    return pl.pallas_call(
        after_kernel,
        out_shape=jax.ShapeDtypeStruct((2,), jnp.int32),
        in_specs=[pl.BlockSpec(memory_space=pl.ANY), scalars],
        out_specs=scalars,
        compiler_params=pltpu.CompilerParams(vmem_limit_bytes=1 << 20),
        cost_estimate=pl.CostEstimate(flops=WIDE, bytes_accessed=64, transcendentals=0),
    )(arrived, where)


def screen_kernel(where, p_ref, b_ref, c_ref, o_ref):
    polar = p_ref[...].reshape(M, M)
    inner = dot(polar, c_ref[...], 1, 1).astype(BF16)
    outer = dot(c_ref[...], inner, 1, 0)
    across = b_ref[...].reshape(M, M).astype(F32)
    o_ref[...] = outer + jnp.where(where[1] > 0, 0.5 * across, 0.0)


def screen(where, got, block):
    return pl.pallas_call(
        screen_kernel,
        out_shape=jax.ShapeDtypeStruct((2, M, M), F32),
        grid_spec=pltpu.PrefetchScalarGridSpec(
            num_scalar_prefetch=1,
            grid=(2,),
            in_specs=[
                pl.BlockSpec((ENERGY, None, None, ROWS, M), lambda w, f: (0, f[0], w, 0, 0)),
                pl.BlockSpec((ENERGY, None, None, ROWS, M), lambda w, f: (0, 1 - f[0], w, 0, 0)),
                pl.BlockSpec((M, M), lambda w, f: (0, 0)),
            ],
            out_specs=pl.BlockSpec((None, M, M), lambda w, f: (w, 0, 0)),
        ),
        compiler_params=pltpu.CompilerParams(vmem_limit_bytes=16 << 20),
        cost_estimate=pl.CostEstimate(flops=8 * M**3, bytes_accessed=9 << 19, transcendentals=0),
    )(where, got, got, block)


def finish_kernel(s_ref, p_ref, o_ref):
    beside = p_ref[...].reshape(M, M).astype(F32)
    o_ref[...] = (s_ref[...] + 0.5 * beside).astype(BF16)


def finish(screened, partner):
    return pl.pallas_call(
        finish_kernel,
        out_shape=jax.ShapeDtypeStruct((2, M, M), BF16),
        grid=(2,),
        in_specs=[
            pl.BlockSpec((None, M, M), lambda w: (w, 0, 0)),
            pl.BlockSpec((ENERGY, None, ROWS, M), lambda w: (0, w, 0, 0)),
        ],
        out_specs=pl.BlockSpec((None, M, M), lambda w: (w, 0, 0)),
        compiler_params=pltpu.CompilerParams(vmem_limit_bytes=16 << 20),
        cost_estimate=pl.CostEstimate(flops=4 * M**2, bytes_accessed=4 << 20, transcendentals=0),
    )(screened, partner)


def to_rows(blocks):
    groups = [[at(e, s) for e in Z_FIRST] for s in range(SLABS)]
    return lax.all_to_all(blocks, BOTH, 0, 0, axis_index_groups=groups, tiled=True)


def tables(count):
    energies = jnp.array([2 * e + k for e in Z_FIRST for k in range(2)], dtype=jnp.int32)
    product = jnp.arange(count, dtype=jnp.int32)[:, None] * energies[None, :] % count
    angles = product.astype(F32) * (2.0 * math.pi / count)
    return (jnp.cos(angles), jnp.sin(angles))


def correlate(rows):
    cosine, sine = tables(NE)
    flat = rows.astype(F32).reshape(NE, -1)
    cosine_part = jnp.dot(cosine, flat, precision=lax.Precision.HIGH)
    sine_part = jnp.dot(sine, flat, precision=lax.Precision.HIGH)
    spectrum = cosine_part * cosine_part + sine_part * sine_part
    folded = jnp.dot(cosine.T, spectrum, precision=lax.Precision.HIGH) * (
        1.0 / (NE * math.sqrt(NE))
    )
    return folded.reshape(rows.shape).astype(BF16)


def on_device(green_blocks, coupling, coulomb):
    green, link, block = green_blocks[:, 0], coupling[0], coulomb[0]
    slab = lax.axis_index("slab")
    own = 1 - (slab & 1)
    across = jnp.where((slab > 0) & (slab < SLABS - 1), 1, 0)
    where = jnp.stack([own, across]).astype(jnp.int32)

    green_above = along_slabs(green, -1)
    rows = to_rows(by_rows(green))
    rows, lower_here, upper, where = lax.optimization_barrier(
        (rows, dress_lower(green, link), dress_upper(green_above, link), where)
    )
    lower = along_slabs(lower_here, 1)
    polar_rows = correlate(rows.reshape(NE, ROWS, M))
    got = home_and_across(polar_rows.reshape(ENERGY, 2, ROWS, M))
    sigma = added(lower, upper)
    got, sigma, where = lax.optimization_barrier((got, sigma, after(lower, where)))
    partner = on_chip(lax.dynamic_index_in_dim(got, own, 1, False))
    screened = finish(screen(where, got, block), partner)
    return (sigma[:, None], screened[:, None])


def solution(mesh):
    placed = (P("energy", "slab", None, None), P("slab", None, None), P("slab", None, None))
    return jax.shard_map(
        on_device,
        mesh=mesh,
        in_specs=placed,
        out_specs=(P("energy", "slab", None, None), P("energy", "slab", None, None)),
        check_vma=False,
    )
```
